128 devices in a mesh: ctx: 8 (over z, core), tp: 16 (over x, y).
Axes of the slice: x: 4, y: 4, z: 4, core: 2. Of those that a mesh axis runs over, the one named last changes fastest.
Arguments:
- inputs: bfloat16 [2048, 8192], P(('ctx', 'tp')), may hold values from -6 to 6
- query_weight: bfloat16 [8192, 8192], P(None, 'tp'), may hold values from -0.0625 to 0.0625
- key_weight: bfloat16 [8192, 8192], P(None, 'tp'), may hold values from -0.0625 to 0.0625
- value_weight: bfloat16 [8192, 8192], P(None, 'tp'), may hold values from -0.0625 to 0.0625
- filter_taps: float32 [128, 8192], P(None, 'tp'), may hold values from -0.45 to 0.45
- out_grad: bfloat16 [2048, 8192], P('ctx', 'tp'), may hold values from -1.5 to 1.5
Outputs:
- mixed: bfloat16 [2048, 8192], P('ctx', 'tp')
- inputs_grad: bfloat16 [2048, 8192], P(('ctx', 'tp'))
- filter_grad: float32 [128, 8192], P(None, 'tp')
The draws below stay inside these ranges and needn't reach their ends.
All inputs are finite; a program needn't handle non-finite values.
Results may differ from the reference program's by a relative error of at most 0.025.
Values may be sent and summed in bfloat16 or wider, within the bound.
A program may use at most 128 MiB of HBM per device.

```python
import jax
import jax.numpy as jnp
from jax import lax

D = 8192
TAPS = 128
TOKENS = 2048
N_TP = 16


def block_levels(own_key, dims, split, low, high):
    level = 1.0
    for dim, shards_of in split:
        steps = jax.random.uniform(jax.random.fold_in(jax.random.fold_in(own_key, 6), dim), (shards_of,), jnp.float32, low / len(split), high / len(split))
        level = level * jnp.repeat(jnp.exp(steps), dims[dim] // shards_of).reshape((-1,) + (1,) * (len(dims) - 1 - dim))
    return level


def noise(own_key, dims, scale, most, pieces=(), held_as=jnp.bfloat16):
    values = jax.random.normal(own_key, dims, jnp.float32) * scale
    if len(pieces) > 0:
        values = block_levels(own_key, dims, pieces, -0.22, 0.18) * values
    return jnp.clip(values, min=-most, max=most).astype(held_as)


def setup_inputs(seed: int = 0) -> dict:
    streams_of = jax.random.split(jax.random.key(seed), 7)
    inputs = noise(streams_of[0], (TOKENS, D), 1.0, 6.0, ((0, 128),))
    query_weight = noise(streams_of[1], (D, D), D ** -0.5, 0.0625, ((1, 16),))
    key_weight = noise(streams_of[2], (D, D), D ** -0.5, 0.0625, ((1, 16),))
    value_weight = noise(streams_of[3], (D, D), D ** -0.5, 0.0625, ((1, 16),))
    filter_taps = noise(streams_of[4], (TAPS, D), 0.09, 0.45, ((1, 16),), jnp.float32)
    out_grad = noise(streams_of[5], (TOKENS, D), 0.25, 1.5, ((0, 8), (1, 16)))
    return {"inputs": inputs, "query_weight": query_weight, "key_weight": key_weight, "value_weight": value_weight, "filter_taps": filter_taps, "out_grad": out_grad}


def forward_filter(padded, filter_taps, length):
    taps = filter_taps.shape[0]
    total = jnp.zeros((length, padded.shape[1]), jnp.float32)
    for offset in range(taps):
        start = taps - 1 - offset
        total = total + filter_taps[offset] * padded[start:start + length]
    return total


def backward_filter(padded, filter_taps, length):
    taps = filter_taps.shape[0]
    total = jnp.zeros((length, padded.shape[1]), jnp.float32)
    for offset in range(taps):
        total = total + filter_taps[offset] * padded[offset:offset + length]
    return total


def tap_products(grad_rows, padded, taps, length):
    rows_out = []
    for offset in range(taps):
        start = taps - 1 - offset
        rows_out.append(jnp.sum(grad_rows * padded[start:start + length], axis=0))
    return jnp.stack(rows_out)


def reference(inputs, query_weight, key_weight, value_weight, filter_taps, out_grad):
    length = inputs.shape[0]
    width = inputs.shape[1]
    taps = filter_taps.shape[0]
    margin = taps - 1
    query = jnp.dot(inputs, query_weight, preferred_element_type=jnp.float32).astype(jnp.bfloat16)
    keys = jnp.dot(inputs, key_weight, preferred_element_type=jnp.float32).astype(jnp.bfloat16)
    values = jnp.dot(inputs, value_weight, preferred_element_type=jnp.float32).astype(jnp.bfloat16)
    product = (keys.astype(jnp.float32) * values.astype(jnp.float32)).astype(jnp.bfloat16)
    padded_prod = jnp.concatenate([jnp.zeros((margin, width), jnp.float32), product.astype(jnp.float32)], axis=0)
    conv = forward_filter(padded_prod, filter_taps, length)
    mixed = (query.astype(jnp.float32) * conv).astype(jnp.bfloat16)
    grad_f32 = out_grad.astype(jnp.float32)
    conv_in_grad = (grad_f32 * query.astype(jnp.float32)).astype(jnp.bfloat16)
    query_grad = (grad_f32 * conv).astype(jnp.bfloat16)
    padded_grad = jnp.concatenate([conv_in_grad.astype(jnp.float32), jnp.zeros((margin, width), jnp.float32)], axis=0)
    product_grad = backward_filter(padded_grad, filter_taps, length)
    keys_grad = (product_grad * values.astype(jnp.float32)).astype(jnp.bfloat16)
    values_grad = (product_grad * keys.astype(jnp.float32)).astype(jnp.bfloat16)
    filter_grad = tap_products(conv_in_grad.astype(jnp.float32), padded_prod, taps, length)
    group = width // N_TP

    def columns(array, index):
        return lax.dynamic_slice_in_dim(array, index * group, group, 1)

    def contract(left, right):
        return lax.dot_general(left, right, (((1,), (1,)), ((), ())), preferred_element_type=jnp.float32)

    def add_group(index, total):
        partial_sum = contract(columns(query_grad, index), columns(query_weight, index))
        partial_sum = partial_sum + contract(columns(keys_grad, index), columns(key_weight, index))
        partial_sum = partial_sum + contract(columns(values_grad, index), columns(value_weight, index))
        rounded = lax.optimization_barrier(partial_sum.astype(jnp.bfloat16))
        return total + rounded.astype(jnp.float32)

    summed = lax.fori_loop(0, N_TP, add_group, jnp.zeros((length, width), jnp.float32))
    return mixed, summed.astype(jnp.bfloat16), filter_grad
```

```python
import jax
import jax.numpy as jnp
import numpy as np
from jax import lax
from jax.experimental import pallas as pl
from jax.experimental.pallas import tpu as pltpu
from jax.sharding import PartitionSpec as P

MESH = pl.DeviceIdType.MESH
BF, F32 = jnp.bfloat16, jnp.float32
SIDE = 4
ROWS = 16
D = 8192
GROUP = 512
BLOCK = 256
TAPS = 128
N_CTX = 8
FREQ = 192
POINTS = 2 * FREQ
GATHER = (2048, 2048, 1536, 1536, 512, 512)
SCATTER = (512, 512, 1024, 1024, 1024, 1024, 1024, 1024, 512, 512)


def starts(widths):
    return [sum(widths[:i]) for i in range(len(widths))]


def transforms():
    angle = np.pi / POINTS * np.outer(2 * np.arange(FREQ) + 1, np.arange(POINTS))
    forward = np.concatenate([np.cos(angle), -np.sin(angle)], axis=0)
    back = forward.T * (2.0 / POINTS)
    lags = TAPS - np.arange(TAPS)
    inverse = np.concatenate([back[TAPS:], back[:BLOCK], back[lags]], axis=0)
    return jnp.asarray(forward, BF), jnp.asarray(inverse, BF)


def dot(a, b):
    return jnp.dot(a, b, preferred_element_type=F32)


def kernel(
    inp, wq, wk, wv, taps_in, og_in, fwd_in, inv_in,
    mixed_out, grad_out, filt_out,
    X, W, acc, og, taps, fm, im, qkv, prod, cig, hx, hc, xs, hs, co, cs, conv, G,
    mixed, PB, R1H, R1, R2H, R2, gout, fpart, FR, FO,
    own_sem, w_sem, in_sem, out_sem, ag_send, ag_recv, halo_send, halo_recv, rs_send, rs_recv,
    f_send, f_recv,
):
    ctx = lax.axis_index("ctx")
    tp = lax.axis_index("tp")
    x = tp // SIDE
    y = tp % SIDE

    def coord(dim, shift=0):
        return ((x if dim == 0 else y) + shift) % SIDE

    def near(dim, d):
        s = 1 if d == 0 else SIDE - 1
        if dim == 0:
            return {"tp": coord(0, s) * SIDE + y}
        return {"tp": x * SIDE + coord(1, s)}

    own_copies = [pltpu.make_async_copy(inp, X.at[x, y], own_sem)]
    loads = []
    for s, c0 in enumerate(starts(GATHER)):
        cols = pl.ds(c0, GATHER[s])
        loads.append([
            pltpu.make_async_copy(w.at[cols, :], W.at[i, cols, :], w_sem.at[s, i])
            for i, w in enumerate((wq, wk, wv))
        ])
    small = [
        pltpu.make_async_copy(src, dst, in_sem.at[i])
        for i, (src, dst) in enumerate(((fwd_in, fm), (taps_in, taps), (inv_in, im), (og_in, og)))
    ]
    own_copies[0].start()
    for group in loads:
        for c in group:
            c.start()
    for c in small:
        c.start()

    barrier = pltpu.get_barrier_semaphore()
    for dim in range(2):
        for d in range(2):
            pl.semaphore_signal(barrier, inc=1, device_id=near(dim, d), device_id_type=MESH)
    for k in range(1, N_CTX):
        pl.semaphore_signal(barrier, inc=1, device_id={"ctx": (ctx + k) % N_CTX}, device_id_type=MESH)
    pl.semaphore_wait(barrier, 4 + N_CTX - 1)
    own_copies[0].wait()

    def gather_copy(s, kind, d):
        t = s % 2
        c0, kw = starts(GATHER)[s], GATHER[s]
        whole, half = pl.ds(c0, kw), pl.ds(c0 + d * (kw // 2), kw // 2)
        back = SIDE - 1 if d == 0 else 1
        if kind == 0:
            ref, dim = X.at[x, y, :, whole], t
        elif kind == 1:
            c = coord(t, back)
            ref, dim = (X.at[c, y, :, half] if t == 0 else X.at[x, c, :, half]), t
        elif kind == 2:
            ref, dim = (X.at[:, y, :, whole] if t == 0 else X.at[x, :, :, whole]), 1 - t
        else:
            c = coord(1 - t, back)
            ref, dim = (X.at[:, c, :, half] if t == 0 else X.at[c, :, :, half]), 1 - t
        return pltpu.make_async_remote_copy(
            src_ref=ref, dst_ref=ref, send_sem=ag_send.at[s, kind, d], recv_sem=ag_recv.at[s, kind, d],
            device_id=near(dim, d), device_id_type=MESH,
        )

    def gather_stage(s, kind):
        for d in range(2):
            if kind in (1, 3):
                gather_copy(s, kind - 1, d).wait_recv()
            gather_copy(s, kind, d).start()

    def gather_wait(s, kind):
        for d in range(2):
            gather_copy(s, kind, d).wait_recv()

    def project(s):
        c0, kw = starts(GATHER)[s], GATHER[s]
        for c in loads[s]:
            c.wait()

        def one(i, carry):
            w = (i + 1) % 3
            part = dot(X[:, :, :, c0 : c0 + kw].reshape(BLOCK, kw), W[w, c0 : c0 + kw, :])
            if s == 0:
                acc[w] = part
            else:
                acc[w] += part
            return carry

        lax.fori_loop(0, 3, one, 0)

    n = len(GATHER)
    for s in range(n):
        gather_stage(s, 0)
    for c in small:
        c.wait()
    tap = taps[...]
    tap_hi = tap.astype(BF)
    tap_lo = (tap - tap_hi.astype(F32)).astype(BF)
    hs[...] = dot(fm[:, :TAPS], tap_hi) + dot(fm[:, :TAPS], tap_lo)
    for s in range(n):
        gather_stage(s, 1)
        if s >= 2:
            gather_wait(s - 2, 1)
            gather_stage(s - 2, 2)
    for s in (n - 2, n - 1):
        gather_wait(s, 1)
        gather_stage(s, 2)
    gather_stage(0, 3)
    gather_stage(1, 3)
    for s in range(n):
        if s + 2 < n:
            gather_stage(s + 2, 3)
        gather_wait(s, 3)
        project(s)

    qkv[1] = acc[1].astype(BF)
    qkv[2] = acc[2].astype(BF)
    prod[...] = (qkv[1].astype(F32) * qkv[2].astype(F32)).astype(BF)
    tail = pltpu.make_async_remote_copy(
        src_ref=prod.at[pl.ds(BLOCK - TAPS, TAPS)], dst_ref=hx, send_sem=halo_send.at[0], recv_sem=halo_recv.at[0],
        device_id={"ctx": (ctx + 1) % N_CTX}, device_id_type=MESH,
    )
    tail.start()
    qkv[0] = acc[0].astype(BF)
    cig[...] = (og[...].astype(F32) * qkv[0].astype(F32)).astype(BF)
    head = pltpu.make_async_remote_copy(
        src_ref=cig.at[pl.ds(0, TAPS)], dst_ref=hc, send_sem=halo_send.at[1], recv_sem=halo_recv.at[1],
        device_id={"ctx": (ctx + N_CTX - 1) % N_CTX}, device_id_type=MESH,
    )
    head.start()
    xs[...] = dot(fm[:, TAPS:], prod[...])
    co[...] = dot(fm[:, :BLOCK], cig[...])
    for s in range(n):
        for kind in range(4):
            for d in range(2):
                gather_copy(s, kind, d).wait_send()

    h_re, h_im = hs.at[pl.ds(0, FREQ)], hs.at[pl.ds(FREQ, FREQ)]
    tail.wait_recv()
    halo = hx[...]
    xs[...] += dot(fm[:, :TAPS], jnp.where(ctx > 0, halo, jnp.zeros_like(halo)))
    x_re, x_im = xs.at[pl.ds(0, FREQ)], xs.at[pl.ds(FREQ, FREQ)]
    spec = jnp.concatenate(
        [x_re[...] * h_re[...] - x_im[...] * h_im[...], x_re[...] * h_im[...] + x_im[...] * h_re[...]], axis=0
    ).astype(BF)
    conv[...] = dot(im[:BLOCK, :], spec)
    G[0] = (og[...].astype(F32) * conv[...]).astype(BF)
    head.wait_recv()
    halo = hc[...]
    cs[...] = co[...] + dot(fm[:, BLOCK:], jnp.where(ctx < N_CTX - 1, halo, jnp.zeros_like(halo)))
    c_re, c_im = cs.at[pl.ds(0, FREQ)], cs.at[pl.ds(FREQ, FREQ)]
    spec = jnp.concatenate(
        [c_re[...] * h_re[...] + c_im[...] * h_im[...], c_im[...] * h_re[...] - c_re[...] * h_im[...]], axis=0
    ).astype(BF)
    back = dot(im[BLOCK : 2 * BLOCK, :], spec)
    G[1] = (back * qkv[2].astype(F32)).astype(BF)
    G[2] = (back * qkv[1].astype(F32)).astype(BF)

    def scatter_copy(s, kind, d):
        t = s % 2
        c0, kw = starts(SCATTER)[s], SCATTER[s]
        whole, half = pl.ds(c0, kw), pl.ds(c0 + d * (kw // 2), kw // 2)
        ahead = 1 if d == 0 else SIDE - 1
        if kind == 0:
            c, dim = coord(1 - t, 2), 1 - t
            src, dst = (PB.at[:, c, :, half] if t == 0 else PB.at[c, :, :, half]), R1H.at[:, :, half]
        elif kind == 1:
            c, dim = coord(1 - t, ahead), 1 - t
            src, dst = (PB.at[:, c, :, whole] if t == 0 else PB.at[c, :, :, whole]), R1.at[d, :, :, whole]
        elif kind == 2:
            c, dim = coord(t, 2), t
            src, dst = (PB.at[c, y, :, half] if t == 0 else PB.at[x, c, :, half]), R2H.at[:, half]
        else:
            c, dim = coord(t, ahead), t
            src, dst = (PB.at[c, y, :, whole] if t == 0 else PB.at[x, c, :, whole]), R2.at[d, :, whole]
        return pltpu.make_async_remote_copy(
            src_ref=src, dst_ref=dst, send_sem=rs_send.at[s, kind, d], recv_sem=rs_recv.at[s, kind, d],
            device_id=near(dim, d), device_id_type=MESH,
        )

    def produce(s):
        c0, kw = starts(SCATTER)[s], SCATTER[s]
        total = None
        for w in range(3):
            part = lax.dot_general(
                G[w], W[w, c0 : c0 + kw, :], (((1,), (1,)), ((), ())), preferred_element_type=F32
            )
            total = part if total is None else total + part
        PB[:, :, :, c0 : c0 + kw] = total.astype(BF).reshape(SIDE, SIDE, ROWS, kw)
        for d in range(2):
            scatter_copy(s, 0, d).start()

    def add_half_block(s):
        t = s % 2
        c0, kw = starts(SCATTER)[s], SCATTER[s]
        for d in range(2):
            half = slice(c0 + d * (kw // 2), c0 + (d + 1) * (kw // 2))
            c = coord(1 - t, 1 if d == 0 else SIDE - 1)
            scatter_copy(s, 0, d).wait_recv()
            got = R1H[:, :, half].astype(F32)
            if t == 0:
                PB[:, c, :, half] = (PB[:, c, :, half].astype(F32) + got).astype(BF)
            else:
                PB[c, :, :, half] = (PB[c, :, :, half].astype(F32) + got).astype(BF)
            scatter_copy(s, 1, d).start()

    def add_blocks(s):
        t = s % 2
        c0, kw = starts(SCATTER)[s], SCATTER[s]
        cols = slice(c0, c0 + kw)
        for d in range(2):
            scatter_copy(s, 1, d).wait_recv()
        got = R1[0, :, :, cols].astype(F32) + R1[1, :, :, cols].astype(F32)
        if t == 0:
            PB[:, y, :, cols] = (PB[:, y, :, cols].astype(F32) + got).astype(BF)
        else:
            PB[x, :, :, cols] = (PB[x, :, :, cols].astype(F32) + got).astype(BF)
        for d in range(2):
            scatter_copy(s, 2, d).start()

    def add_half_rows(s):
        t = s % 2
        c0, kw = starts(SCATTER)[s], SCATTER[s]
        for d in range(2):
            half = slice(c0 + d * (kw // 2), c0 + (d + 1) * (kw // 2))
            c = coord(t, 1 if d == 0 else SIDE - 1)
            scatter_copy(s, 2, d).wait_recv()
            got = R2H[:, half].astype(F32)
            if t == 0:
                PB[c, y, :, half] = (PB[c, y, :, half].astype(F32) + got).astype(BF)
            else:
                PB[x, c, :, half] = (PB[x, c, :, half].astype(F32) + got).astype(BF)
            scatter_copy(s, 3, d).start()

    def finish(s):
        c0, kw = starts(SCATTER)[s], SCATTER[s]
        cols = slice(c0, c0 + kw)
        for d in range(2):
            scatter_copy(s, 3, d).wait_recv()
        gout[:, cols] = (
            PB[x, y, :, cols].astype(F32) + R2[0, :, cols].astype(F32) + R2[1, :, cols].astype(F32)
        ).astype(BF)

    def piece_copy(k):
        to = (ctx + k) % N_CTX
        return pltpu.make_async_remote_copy(
            src_ref=fpart.at[to], dst_ref=FR.at[k], send_sem=f_send.at[0, k], recv_sem=f_recv.at[0, k],
            device_id={"ctx": to}, device_id_type=MESH,
        )

    def share_copy(k):
        return pltpu.make_async_remote_copy(
            src_ref=FO.at[ctx], dst_ref=FO.at[ctx], send_sem=f_send.at[1, k], recv_sem=f_recv.at[1, k],
            device_id={"ctx": (ctx + k) % N_CTX}, device_id_type=MESH,
        )

    def share_arrival(k):
        slot = (ctx + N_CTX - k) % N_CTX
        return pltpu.make_async_remote_copy(
            src_ref=FO.at[slot], dst_ref=FO.at[slot], send_sem=f_send.at[1, k], recv_sem=f_recv.at[1, k],
            device_id={"ctx": (ctx + k) % N_CTX}, device_id_type=MESH,
        )

    def filter_start():
        o_re, o_im = co.at[pl.ds(0, FREQ)], co.at[pl.ds(FREQ, FREQ)]
        spec = jnp.concatenate(
            [x_re[...] * o_re[...] + x_im[...] * o_im[...], x_im[...] * o_re[...] - x_re[...] * o_im[...]], axis=0
        ).astype(BF)
        fpart[...] = dot(im[2 * BLOCK :, :], spec).reshape(N_CTX, TAPS // N_CTX, GROUP)
        for k in range(1, N_CTX):
            piece_copy(k).start()

    def filter_sum():
        total = fpart[ctx]
        for k in range(1, N_CTX):
            piece_copy(k).wait_recv()
            total = total + FR[k]
        FO[ctx] = total
        for k in range(1, N_CTX):
            share_copy(k).start()

    mixed_copy = pltpu.make_async_copy(mixed, mixed_out, out_sem.at[0])
    m = len(SCATTER)
    lag = 2
    for s in range(m + 4 * lag):
        if s < m:
            produce(s)
        for stage, fn in enumerate((add_half_block, add_blocks, add_half_rows, finish)):
            j = s - (stage + 1) * lag
            if 0 <= j < m:
                fn(j)
        if s == 3:
            filter_start()
        if s == 5:
            mixed[...] = (qkv[0].astype(F32) * conv[...]).astype(BF)
            mixed_copy.start()
        if s == 8:
            filter_sum()
    grad_copy = pltpu.make_async_copy(gout, grad_out, out_sem.at[1])
    grad_copy.start()
    for k in range(1, N_CTX):
        share_arrival(k).wait_recv()
    filt_copy = pltpu.make_async_copy(FO, filt_out, out_sem.at[2])
    filt_copy.start()
    tail.wait_send()
    head.wait_send()
    for s in range(m):
        for kind in range(4):
            for d in range(2):
                scatter_copy(s, kind, d).wait_send()
    for k in range(1, N_CTX):
        piece_copy(k).wait_send()
        share_copy(k).wait_send()
    mixed_copy.wait()
    grad_copy.wait()
    filt_copy.wait()


def on_device(inputs, query_weight, key_weight, value_weight, filter_taps, out_grad):
    forward, inverse = transforms()
    vm, dma = pltpu.VMEM, pltpu.SemaphoreType.DMA
    n, m = len(GATHER), len(SCATTER)
    piece = TAPS // N_CTX
    mixed, grad, filt = pl.pallas_call(
        kernel,
        out_shape=(
            jax.ShapeDtypeStruct((BLOCK, GROUP), BF),
            jax.ShapeDtypeStruct((ROWS, D), BF),
            jax.ShapeDtypeStruct((N_CTX, piece, GROUP), F32),
        ),
        in_specs=[pl.BlockSpec(memory_space=pl.ANY)] * 8,
        out_specs=(pl.BlockSpec(memory_space=pl.ANY),) * 3,
        scratch_shapes=[
            vm((SIDE, SIDE, ROWS, D), BF),
            vm((3, D, GROUP), BF),
            vm((3, BLOCK, GROUP), F32),
            vm((BLOCK, GROUP), BF),
            vm((TAPS, GROUP), F32),
            vm((POINTS, POINTS), BF),
            vm((2 * BLOCK + TAPS, POINTS), BF),
            vm((3, BLOCK, GROUP), BF),
            vm((BLOCK, GROUP), BF),
            vm((BLOCK, GROUP), BF),
            vm((TAPS, GROUP), BF),
            vm((TAPS, GROUP), BF),
            vm((POINTS, GROUP), F32),
            vm((POINTS, GROUP), F32),
            vm((POINTS, GROUP), F32),
            vm((POINTS, GROUP), F32),
            vm((BLOCK, GROUP), F32),
            vm((3, BLOCK, GROUP), BF),
            vm((BLOCK, GROUP), BF),
            vm((SIDE, SIDE, ROWS, D), BF),
            vm((SIDE, ROWS, D), BF),
            vm((2, SIDE, ROWS, D), BF),
            vm((ROWS, D), BF),
            vm((2, ROWS, D), BF),
            vm((ROWS, D), BF),
            vm((N_CTX, piece, GROUP), F32),
            vm((N_CTX, piece, GROUP), F32),
            vm((N_CTX, piece, GROUP), F32),
            dma,
            dma((n, 3)),
            dma((4,)),
            dma((3,)),
            dma((n, 4, 2)),
            dma((n, 4, 2)),
            dma((2,)),
            dma((2,)),
            dma((m, 4, 2)),
            dma((m, 4, 2)),
            dma((2, N_CTX)),
            dma((2, N_CTX)),
        ],
        compiler_params=pltpu.CompilerParams(
            collective_id=0, has_side_effects=True, vmem_limit_bytes=60 << 20
        ),
    )(inputs, query_weight, key_weight, value_weight, filter_taps, out_grad, forward, inverse)
    return mixed, grad, filt.reshape(TAPS, GROUP)


def solution(mesh):
    in_specs = (
        P(("ctx", "tp"), None),
        P(None, "tp"),
        P(None, "tp"),
        P(None, "tp"),
        P(None, "tp"),
        P("ctx", "tp"),
    )
    out_specs = (P("ctx", "tp"), P(("ctx", "tp"), None), P(None, "tp"))
    return jax.shard_map(
        on_device, mesh=mesh, in_specs=in_specs, out_specs=out_specs, check_vma=False
    )
```

```python
import jax
import jax.numpy as jnp
import numpy as np
from jax import lax
from jax.experimental import pallas as pl
from jax.experimental.pallas import tpu as pltpu
from jax.sharding import PartitionSpec as P

MESH = pl.DeviceIdType.MESH
BF, F32 = jnp.bfloat16, jnp.float32
SIDE = 4
ROWS = 16
D = 8192
GROUP = 512
BLOCK = 256
TAPS = 128
N_CTX = 8
FREQ = 192
POINTS = 2 * FREQ
GATHER = (2048, 2048, 2048, 2048)
SCATTER = (1024, 1024, 2048, 2048, 1024, 1024)


def starts(widths):
    return [sum(widths[:i]) for i in range(len(widths))]


def transforms():
    angle = np.pi / POINTS * np.outer(2 * np.arange(FREQ) + 1, np.arange(POINTS))
    forward = np.concatenate([np.cos(angle), -np.sin(angle)], axis=0)
    back = forward.T * (2.0 / POINTS)
    lags = TAPS - np.arange(TAPS)
    inverse = np.concatenate([back[TAPS:], back[:BLOCK], back[lags]], axis=0)
    return jnp.asarray(forward, BF), jnp.asarray(inverse, BF)


def dot(a, b):
    return jnp.dot(a, b, preferred_element_type=F32)


def kernel(
    inp, wq, wk, wv, taps_in, og_in, fwd_in, inv_in,
    mixed_out, grad_out, filt_out,
    X, W, acc, og, taps, fm, im, qkv, prod, cig, hx, hc, xs, hs, co, cs, conv, G,
    mixed, PB, R1H, R1, R2H, R2, gout, fpart, FR, FO,
    own_sem, w_sem, in_sem, out_sem, ag_send, ag_recv, halo_send, halo_recv, rs_send, rs_recv,
    f_send, f_recv, met,
):
    ctx = lax.axis_index("ctx")
    tp = lax.axis_index("tp")
    x = tp // SIDE
    y = tp % SIDE

    def coord(dim, shift=0):
        return ((x if dim == 0 else y) + shift) % SIDE

    def near(dim, d):
        s = 1 if d == 0 else SIDE - 1
        if dim == 0:
            return {"tp": coord(0, s) * SIDE + y}
        return {"tp": x * SIDE + coord(1, s)}

    own_copies = [pltpu.make_async_copy(inp, X.at[x, y], own_sem)]
    loads = []
    for s, c0 in enumerate(starts(GATHER)):
        cols = pl.ds(c0, GATHER[s])
        loads.append([
            pltpu.make_async_copy(w.at[cols, :], W.at[i, cols, :], w_sem.at[s, i])
            for i, w in enumerate((wq, wk, wv))
        ])
    small = [
        pltpu.make_async_copy(src, dst, in_sem.at[i])
        for i, (src, dst) in enumerate(((fwd_in, fm), (taps_in, taps), (inv_in, im), (og_in, og)))
    ]
    own_copies[0].start()

    barrier = pltpu.get_barrier_semaphore()
    for dim in range(2):
        for d in range(2):
            pl.semaphore_signal(barrier, inc=1, device_id=near(dim, d), device_id_type=MESH)
    along = ({"ctx": (ctx + 1) % N_CTX}, {"ctx": (ctx + N_CTX - 1) % N_CTX})
    for to in along:
        pl.semaphore_signal(barrier, inc=1, device_id=to, device_id_type=MESH)
    pl.semaphore_wait(barrier, 6)

    def greet(r):
        for d, to in enumerate(along):
            pl.semaphore_signal(met.at[r, d], inc=1, device_id=to, device_id_type=MESH)

    def greeted(r):
        for d in range(2):
            pl.semaphore_wait(met.at[r, d], 1)

    own_copies[0].wait()

    def gather_copy(s, kind, d):
        t = s % 2
        c0, kw = starts(GATHER)[s], GATHER[s]
        whole, half = pl.ds(c0, kw), pl.ds(c0 + d * (kw // 2), kw // 2)
        back = SIDE - 1 if d == 0 else 1
        if kind == 0:
            ref, dim = X.at[x, y, :, whole], t
        elif kind == 1:
            c = coord(t, back)
            ref, dim = (X.at[c, y, :, half] if t == 0 else X.at[x, c, :, half]), t
        elif kind == 2:
            ref, dim = (X.at[:, y, :, whole] if t == 0 else X.at[x, :, :, whole]), 1 - t
        else:
            c = coord(1 - t, back)
            ref, dim = (X.at[:, c, :, half] if t == 0 else X.at[c, :, :, half]), 1 - t
        return pltpu.make_async_remote_copy(
            src_ref=ref, dst_ref=ref, send_sem=ag_send.at[s, kind, d], recv_sem=ag_recv.at[s, kind, d],
            device_id=near(dim, d), device_id_type=MESH,
        )

    def gather_stage(s, kind):
        for d in range(2):
            if kind in (1, 3):
                gather_copy(s, kind - 1, d).wait_recv()
            gather_copy(s, kind, d).start()

    def gather_wait(s, kind):
        for d in range(2):
            gather_copy(s, kind, d).wait_recv()

    def project(s):
        c0, kw = starts(GATHER)[s], GATHER[s]
        for c in loads[s]:
            c.wait()

        def one(i, carry):
            w = (i + 1) % 3
            part = dot(X[:, :, :, c0 : c0 + kw].reshape(BLOCK, kw), W[w, c0 : c0 + kw, :])
            if s == 0:
                acc[w] = part
            else:
                acc[w] += part
            return carry

        lax.fori_loop(0, 3, one, 0)

    n = len(GATHER)
    for s in range(n):
        gather_stage(s, 0)
    greet(0)
    for c in small:
        c.start()
    for group in loads:
        for c in group:
            c.start(priority=1)
    for c in small:
        c.wait()
    tap = taps[...]
    tap_hi = tap.astype(BF)
    tap_lo = (tap - tap_hi.astype(F32)).astype(BF)
    hs[...] = dot(fm[:, :TAPS], tap_hi) + dot(fm[:, :TAPS], tap_lo)
    for s in range(n):
        gather_stage(s, 1)
        if s >= 2:
            gather_wait(s - 2, 1)
            gather_stage(s - 2, 2)
    for s in (n - 2, n - 1):
        gather_wait(s, 1)
        gather_stage(s, 2)
    greeted(0)
    greet(1)
    gather_stage(0, 3)
    gather_stage(1, 3)
    greeted(1)
    greet(2)
    for s in range(n):
        if s + 2 < n:
            gather_stage(s + 2, 3)
        gather_wait(s, 3)
        project(s)

    greeted(2)

    qkv[1] = acc[1].astype(BF)
    qkv[2] = acc[2].astype(BF)
    prod[...] = (qkv[1].astype(F32) * qkv[2].astype(F32)).astype(BF)
    tail = pltpu.make_async_remote_copy(
        src_ref=prod.at[pl.ds(BLOCK - TAPS, TAPS)], dst_ref=hx, send_sem=halo_send.at[0], recv_sem=halo_recv.at[0],
        device_id={"ctx": (ctx + 1) % N_CTX}, device_id_type=MESH,
    )
    tail.start()
    qkv[0] = acc[0].astype(BF)
    cig[...] = (og[...].astype(F32) * qkv[0].astype(F32)).astype(BF)
    head = pltpu.make_async_remote_copy(
        src_ref=cig.at[pl.ds(0, TAPS)], dst_ref=hc, send_sem=halo_send.at[1], recv_sem=halo_recv.at[1],
        device_id={"ctx": (ctx + N_CTX - 1) % N_CTX}, device_id_type=MESH,
    )
    head.start()
    xs[...] = dot(fm[:, TAPS:], prod[...])
    co[...] = dot(fm[:, :BLOCK], cig[...])
    for s in range(n):
        for kind in range(4):
            for d in range(2):
                gather_copy(s, kind, d).wait_send()

    h_re, h_im = hs.at[pl.ds(0, FREQ)], hs.at[pl.ds(FREQ, FREQ)]
    tail.wait_recv()
    halo = hx[...]
    xs[...] += dot(fm[:, :TAPS], jnp.where(ctx > 0, halo, jnp.zeros_like(halo)))
    x_re, x_im = xs.at[pl.ds(0, FREQ)], xs.at[pl.ds(FREQ, FREQ)]
    spec = jnp.concatenate(
        [x_re[...] * h_re[...] - x_im[...] * h_im[...], x_re[...] * h_im[...] + x_im[...] * h_re[...]], axis=0
    ).astype(BF)
    conv[...] = dot(im[:BLOCK, :], spec)
    G[0] = (og[...].astype(F32) * conv[...]).astype(BF)
    head.wait_recv()
    halo = hc[...]
    cs[...] = co[...] + dot(fm[:, BLOCK:], jnp.where(ctx < N_CTX - 1, halo, jnp.zeros_like(halo)))
    c_re, c_im = cs.at[pl.ds(0, FREQ)], cs.at[pl.ds(FREQ, FREQ)]
    spec = jnp.concatenate(
        [c_re[...] * h_re[...] + c_im[...] * h_im[...], c_im[...] * h_re[...] - c_re[...] * h_im[...]], axis=0
    ).astype(BF)
    back = dot(im[BLOCK : 2 * BLOCK, :], spec)
    G[1] = (back * qkv[2].astype(F32)).astype(BF)
    G[2] = (back * qkv[1].astype(F32)).astype(BF)

    def scatter_copy(s, kind, d):
        t = s % 2
        c0, kw = starts(SCATTER)[s], SCATTER[s]
        whole, half = pl.ds(c0, kw), pl.ds(c0 + d * (kw // 2), kw // 2)
        ahead = 1 if d == 0 else SIDE - 1
        if kind == 0:
            c, dim = coord(1 - t, 2), 1 - t
            src, dst = (PB.at[:, c, :, half] if t == 0 else PB.at[c, :, :, half]), R1H.at[:, :, half]
        elif kind == 1:
            c, dim = coord(1 - t, ahead), 1 - t
            src, dst = (PB.at[:, c, :, whole] if t == 0 else PB.at[c, :, :, whole]), R1.at[d, :, :, whole]
        elif kind == 2:
            c, dim = coord(t, 2), t
            src, dst = (PB.at[c, y, :, half] if t == 0 else PB.at[x, c, :, half]), R2H.at[:, half]
        else:
            c, dim = coord(t, ahead), t
            src, dst = (PB.at[c, y, :, whole] if t == 0 else PB.at[x, c, :, whole]), R2.at[d, :, whole]
        return pltpu.make_async_remote_copy(
            src_ref=src, dst_ref=dst, send_sem=rs_send.at[s, kind, d], recv_sem=rs_recv.at[s, kind, d],
            device_id=near(dim, d), device_id_type=MESH,
        )

    def produce(s):
        c0, kw = starts(SCATTER)[s], SCATTER[s]
        total = None
        for w in range(3):
            part = lax.dot_general(
                G[w], W[w, c0 : c0 + kw, :], (((1,), (1,)), ((), ())), preferred_element_type=F32
            )
            total = part if total is None else total + part
        PB[:, :, :, c0 : c0 + kw] = total.astype(BF).reshape(SIDE, SIDE, ROWS, kw)
        for d in range(2):
            scatter_copy(s, 0, d).start()

    def add_half_block(s):
        t = s % 2
        c0, kw = starts(SCATTER)[s], SCATTER[s]
        for d in range(2):
            half = slice(c0 + d * (kw // 2), c0 + (d + 1) * (kw // 2))
            c = coord(1 - t, 1 if d == 0 else SIDE - 1)
            scatter_copy(s, 0, d).wait_recv()
            got = R1H[:, :, half].astype(F32)
            if t == 0:
                PB[:, c, :, half] = (PB[:, c, :, half].astype(F32) + got).astype(BF)
            else:
                PB[c, :, :, half] = (PB[c, :, :, half].astype(F32) + got).astype(BF)
            scatter_copy(s, 1, d).start()

    def add_blocks(s):
        t = s % 2
        c0, kw = starts(SCATTER)[s], SCATTER[s]
        cols = slice(c0, c0 + kw)
        for d in range(2):
            scatter_copy(s, 1, d).wait_recv()
        got = R1[0, :, :, cols].astype(F32) + R1[1, :, :, cols].astype(F32)
        if t == 0:
            PB[:, y, :, cols] = (PB[:, y, :, cols].astype(F32) + got).astype(BF)
        else:
            PB[x, :, :, cols] = (PB[x, :, :, cols].astype(F32) + got).astype(BF)
        for d in range(2):
            scatter_copy(s, 2, d).start()

    def add_half_rows(s):
        t = s % 2
        c0, kw = starts(SCATTER)[s], SCATTER[s]
        for d in range(2):
            half = slice(c0 + d * (kw // 2), c0 + (d + 1) * (kw // 2))
            c = coord(t, 1 if d == 0 else SIDE - 1)
            scatter_copy(s, 2, d).wait_recv()
            got = R2H[:, half].astype(F32)
            if t == 0:
                PB[c, y, :, half] = (PB[c, y, :, half].astype(F32) + got).astype(BF)
            else:
                PB[x, c, :, half] = (PB[x, c, :, half].astype(F32) + got).astype(BF)
            scatter_copy(s, 3, d).start()

    def finish(s):
        c0, kw = starts(SCATTER)[s], SCATTER[s]
        cols = slice(c0, c0 + kw)
        for d in range(2):
            scatter_copy(s, 3, d).wait_recv()
        gout[:, cols] = (
            PB[x, y, :, cols].astype(F32) + R2[0, :, cols].astype(F32) + R2[1, :, cols].astype(F32)
        ).astype(BF)

    def piece_copy(k):
        to = (ctx + k) % N_CTX
        return pltpu.make_async_remote_copy(
            src_ref=fpart.at[to], dst_ref=FR.at[k], send_sem=f_send.at[0, k], recv_sem=f_recv.at[0, k],
            device_id={"ctx": to}, device_id_type=MESH,
        )

    def share_copy(k):
        return pltpu.make_async_remote_copy(
            src_ref=FO.at[ctx], dst_ref=FO.at[ctx], send_sem=f_send.at[1, k], recv_sem=f_recv.at[1, k],
            device_id={"ctx": (ctx + k) % N_CTX}, device_id_type=MESH,
        )

    def share_arrival(k):
        slot = (ctx + N_CTX - k) % N_CTX
        return pltpu.make_async_remote_copy(
            src_ref=FO.at[slot], dst_ref=FO.at[slot], send_sem=f_send.at[1, k], recv_sem=f_recv.at[1, k],
            device_id={"ctx": (ctx + k) % N_CTX}, device_id_type=MESH,
        )

    def filter_start():
        o_re, o_im = co.at[pl.ds(0, FREQ)], co.at[pl.ds(FREQ, FREQ)]
        spec = jnp.concatenate(
            [x_re[...] * o_re[...] + x_im[...] * o_im[...], x_im[...] * o_re[...] - x_re[...] * o_im[...]], axis=0
        ).astype(BF)
        fpart[...] = dot(im[2 * BLOCK :, :], spec).reshape(N_CTX, TAPS // N_CTX, GROUP)
        for k in range(1, N_CTX):
            piece_copy(k).start()

    def filter_sum():
        total = fpart[ctx]
        for k in range(1, N_CTX):
            piece_copy(k).wait_recv()
            total = total + FR[k]
        FO[ctx] = total
        for k in range(1, N_CTX):
            share_copy(k).start()

    mixed_copy = pltpu.make_async_copy(mixed, mixed_out, out_sem.at[0])
    m = len(SCATTER)
    lag = 2
    for s in range(m + 4 * lag):
        if s < m:
            produce(s)
        for stage, fn in enumerate((add_half_block, add_blocks, add_half_rows, finish)):
            j = s - (stage + 1) * lag
            if 0 <= j < m:
                fn(j)
        if s == 3:
            filter_start()
        if s == 5:
            mixed[...] = (qkv[0].astype(F32) * conv[...]).astype(BF)
            mixed_copy.start()
        if s == 8:
            filter_sum()
    grad_copy = pltpu.make_async_copy(gout, grad_out, out_sem.at[1])
    grad_copy.start()
    for k in range(1, N_CTX):
        share_arrival(k).wait_recv()
    filt_copy = pltpu.make_async_copy(FO, filt_out, out_sem.at[2])
    filt_copy.start()
    tail.wait_send()
    head.wait_send()
    for s in range(m):
        for kind in range(4):
            for d in range(2):
                scatter_copy(s, kind, d).wait_send()
    for k in range(1, N_CTX):
        piece_copy(k).wait_send()
        share_copy(k).wait_send()
    mixed_copy.wait()
    grad_copy.wait()
    filt_copy.wait()


def hand_on(*refs):
    held, load_sem, store_sem = refs[6:9], refs[9], refs[10]
    loads = [pltpu.make_async_copy(refs[i], held[i], load_sem.at[i]) for i in range(3)]
    stores = [pltpu.make_async_copy(held[i], refs[3 + i], store_sem.at[i]) for i in range(3)]
    for c in loads:
        c.start()
    for i in range(3):
        loads[i].wait()
        stores[i].start()
    for c in stores:
        c.wait()


def on_device(inputs, query_weight, key_weight, value_weight, filter_taps, out_grad):
    forward, inverse = transforms()
    vm, dma = pltpu.VMEM, pltpu.SemaphoreType.DMA
    n, m = len(GATHER), len(SCATTER)
    piece = TAPS // N_CTX
    mixed, grad, filt = pl.pallas_call(
        kernel,
        out_shape=(
            jax.ShapeDtypeStruct((BLOCK, GROUP), BF),
            jax.ShapeDtypeStruct((ROWS, D), BF),
            jax.ShapeDtypeStruct((N_CTX, piece, GROUP), F32),
        ),
        in_specs=[pl.BlockSpec(memory_space=pl.ANY)] * 8,
        out_specs=(pl.BlockSpec(memory_space=pl.ANY),) * 3,
        scratch_shapes=[
            vm((SIDE, SIDE, ROWS, D), BF),
            vm((3, D, GROUP), BF),
            vm((3, BLOCK, GROUP), F32),
            vm((BLOCK, GROUP), BF),
            vm((TAPS, GROUP), F32),
            vm((POINTS, POINTS), BF),
            vm((2 * BLOCK + TAPS, POINTS), BF),
            vm((3, BLOCK, GROUP), BF),
            vm((BLOCK, GROUP), BF),
            vm((BLOCK, GROUP), BF),
            vm((TAPS, GROUP), BF),
            vm((TAPS, GROUP), BF),
            vm((POINTS, GROUP), F32),
            vm((POINTS, GROUP), F32),
            vm((POINTS, GROUP), F32),
            vm((POINTS, GROUP), F32),
            vm((BLOCK, GROUP), F32),
            vm((3, BLOCK, GROUP), BF),
            vm((BLOCK, GROUP), BF),
            vm((SIDE, SIDE, ROWS, D), BF),
            vm((SIDE, ROWS, D), BF),
            vm((2, SIDE, ROWS, D), BF),
            vm((ROWS, D), BF),
            vm((2, ROWS, D), BF),
            vm((ROWS, D), BF),
            vm((N_CTX, piece, GROUP), F32),
            vm((N_CTX, piece, GROUP), F32),
            vm((N_CTX, piece, GROUP), F32),
            dma,
            dma((n, 3)),
            dma((4,)),
            dma((3,)),
            dma((n, 4, 2)),
            dma((n, 4, 2)),
            dma((2,)),
            dma((2,)),
            dma((m, 4, 2)),
            dma((m, 4, 2)),
            dma((2, N_CTX)),
            dma((2, N_CTX)),
            pltpu.SemaphoreType.REGULAR((3, 2)),
        ],
        compiler_params=pltpu.CompilerParams(
            collective_id=0, has_side_effects=True, vmem_limit_bytes=60 << 20
        ),
    )(inputs, query_weight, key_weight, value_weight, filter_taps, out_grad, forward, inverse)
    outs = (mixed, grad, filt.reshape(TAPS, GROUP))
    return pl.pallas_call(
        hand_on,
        out_shape=tuple(jax.ShapeDtypeStruct(v.shape, v.dtype) for v in outs),
        in_specs=[pl.BlockSpec(memory_space=pl.ANY)] * 3,
        out_specs=(pl.BlockSpec(memory_space=pl.ANY),) * 3,
        scratch_shapes=[*(vm(v.shape, v.dtype) for v in outs), dma((3,)), dma((3,))],
    )(*outs)


def solution(mesh):
    in_specs = (
        P(("ctx", "tp"), None),
        P(None, "tp"),
        P(None, "tp"),
        P(None, "tp"),
        P(None, "tp"),
        P("ctx", "tp"),
    )
    out_specs = (P("ctx", "tp"), P(("ctx", "tp"), None), P(None, "tp"))
    return jax.shard_map(
        on_device, mesh=mesh, in_specs=in_specs, out_specs=out_specs, check_vma=False
    )
```

```python
import jax
import jax.numpy as jnp
import numpy as np
from jax import lax
from jax.experimental import pallas as pl
from jax.experimental.pallas import tpu as pltpu
from jax.sharding import PartitionSpec as P

MESH = pl.DeviceIdType.MESH
BF, F32 = jnp.bfloat16, jnp.float32
SIDE = 4
ROWS = 16
D = 8192
GROUP = 512
BLOCK = 256
TAPS = 128
N_CTX = 8
FREQ = 192
POINTS = 2 * FREQ
GATHER = (2048, 2048, 2048, 2048)
SCATTER = (1024, 1024, 2048, 2048, 1024, 1024)


def starts(widths):
    return [sum(widths[:i]) for i in range(len(widths))]


def transforms():
    angle = np.pi / POINTS * np.outer(2 * np.arange(FREQ) + 1, np.arange(POINTS))
    forward = np.concatenate([np.cos(angle), -np.sin(angle)], axis=0)
    back = forward.T * (2.0 / POINTS)
    lags = TAPS - np.arange(TAPS)
    inverse = np.concatenate([back[TAPS:], back[:BLOCK], back[lags]], axis=0)
    return jnp.asarray(forward, BF), jnp.asarray(inverse, BF)


def dot(a, b):
    return jnp.dot(a, b, preferred_element_type=F32)


def kernel(
    inp, wq, wk, wv, taps_in, og_in, fwd_in, inv_in,
    mixed_out, grad_out, filt_out,
    X, W, acc, og, taps, fm, im, qkv, prod, cig, hx, hc, xs, hs, co, cs, conv, G,
    mixed, PB, R1H, R1, R2H, R2, gout, fpart, FR, FO, fout,
    own_sem, w_sem, in_sem, out_sem, ag_send, ag_recv, halo_send, halo_recv, rs_send, rs_recv,
    f_send, f_recv, met,
):
    ctx = lax.axis_index("ctx")
    tp = lax.axis_index("tp")
    x = tp // SIDE
    y = tp % SIDE

    def coord(dim, shift=0):
        return ((x if dim == 0 else y) + shift) % SIDE

    def near(dim, d):
        s = 1 if d == 0 else SIDE - 1
        if dim == 0:
            return {"tp": coord(0, s) * SIDE + y}
        return {"tp": x * SIDE + coord(1, s)}

    own_copies = [pltpu.make_async_copy(inp, X.at[x, y], own_sem)]
    loads = []
    for s, c0 in enumerate(starts(GATHER)):
        cols = pl.ds(c0, GATHER[s])
        loads.append([
            pltpu.make_async_copy(w.at[cols, :], W.at[i, cols, :], w_sem.at[s, i])
            for i, w in enumerate((wq, wk, wv))
        ])
    small = [
        pltpu.make_async_copy(src, dst, in_sem.at[i])
        for i, (src, dst) in enumerate(((fwd_in, fm), (taps_in, taps), (inv_in, im), (og_in, og)))
    ]
    own_copies[0].start()
    for c in small:
        c.start(priority=1)

    barrier = pltpu.get_barrier_semaphore()
    for dim in range(2):
        for d in range(2):
            pl.semaphore_signal(barrier, inc=1, device_id=near(dim, d), device_id_type=MESH)
    along = ({"ctx": (ctx + 1) % N_CTX}, {"ctx": (ctx + N_CTX - 1) % N_CTX})
    for to in along:
        pl.semaphore_signal(barrier, inc=1, device_id=to, device_id_type=MESH)
    pl.semaphore_wait(barrier, 6)

    def greet(r):
        for d, to in enumerate(along):
            pl.semaphore_signal(met.at[r, d], inc=1, device_id=to, device_id_type=MESH)

    def greeted(r):
        for d in range(2):
            pl.semaphore_wait(met.at[r, d], 1)

    own_copies[0].wait()

    def gather_copy(s, kind, d):
        t = s % 2
        c0, kw = starts(GATHER)[s], GATHER[s]
        whole, half = pl.ds(c0, kw), pl.ds(c0 + d * (kw // 2), kw // 2)
        back = SIDE - 1 if d == 0 else 1
        if kind == 0:
            ref, dim = X.at[x, y, :, whole], t
        elif kind == 1:
            c = coord(t, back)
            ref, dim = (X.at[c, y, :, half] if t == 0 else X.at[x, c, :, half]), t
        elif kind == 2:
            ref, dim = (X.at[:, y, :, whole] if t == 0 else X.at[x, :, :, whole]), 1 - t
        else:
            c = coord(1 - t, back)
            ref, dim = (X.at[:, c, :, half] if t == 0 else X.at[c, :, :, half]), 1 - t
        return pltpu.make_async_remote_copy(
            src_ref=ref, dst_ref=ref, send_sem=ag_send.at[s, kind, d], recv_sem=ag_recv.at[s, kind, d],
            device_id=near(dim, d), device_id_type=MESH,
        )

    def gather_stage(s, kind):
        for d in range(2):
            if kind in (1, 3):
                gather_copy(s, kind - 1, d).wait_recv()
            gather_copy(s, kind, d).start()

    def gather_wait(s, kind):
        for d in range(2):
            gather_copy(s, kind, d).wait_recv()

    def project(s, first, last):
        c0, kw = starts(GATHER)[s], GATHER[s]

        def one(w, carry):
            part = dot(X[:, :, :, c0 : c0 + kw].reshape(BLOCK, kw), W[w, c0 : c0 + kw, :])
            if s == 0:
                acc[w] = part
            else:
                acc[w] += part
            return carry

        lax.fori_loop(first, last, one, 0)

    n = len(GATHER)
    for s in range(n):
        gather_stage(s, 0)
    greet(0)
    for group in loads:
        for c in group:
            c.start(priority=1)
    for s in range(n):
        gather_stage(s, 1)
        if s >= 2:
            gather_wait(s - 2, 1)
            gather_stage(s - 2, 2)
    for s in (n - 2, n - 1):
        gather_wait(s, 1)
        gather_stage(s, 2)
    greeted(0)
    greet(1)
    for c in small:
        c.wait()
    tap = taps[...]
    tap_hi = tap.astype(BF)
    tap_lo = (tap - tap_hi.astype(F32)).astype(BF)
    hs[...] = dot(fm[:, :TAPS], tap_hi) + dot(fm[:, :TAPS], tap_lo)
    gather_stage(0, 3)
    gather_stage(1, 3)
    greeted(1)
    greet(2)
    for s in range(n):
        if s + 2 < n:
            gather_stage(s + 2, 3)
        gather_wait(s, 3)
        for c in loads[s]:
            c.wait()
        project(s, 0 if s < n - 2 else 1, 3)

    greeted(2)

    qkv[1] = acc[1].astype(BF)
    qkv[2] = acc[2].astype(BF)
    prod[...] = (qkv[1].astype(F32) * qkv[2].astype(F32)).astype(BF)
    tail = pltpu.make_async_remote_copy(
        src_ref=prod.at[pl.ds(BLOCK - TAPS, TAPS)], dst_ref=hx, send_sem=halo_send.at[0], recv_sem=halo_recv.at[0],
        device_id={"ctx": (ctx + 1) % N_CTX}, device_id_type=MESH,
    )
    tail.start()
    for s in (n - 2, n - 1):
        project(s, 0, 1)
    qkv[0] = acc[0].astype(BF)
    cig[...] = (og[...].astype(F32) * qkv[0].astype(F32)).astype(BF)
    head = pltpu.make_async_remote_copy(
        src_ref=cig.at[pl.ds(0, TAPS)], dst_ref=hc, send_sem=halo_send.at[1], recv_sem=halo_recv.at[1],
        device_id={"ctx": (ctx + N_CTX - 1) % N_CTX}, device_id_type=MESH,
    )
    head.start()
    xs[...] = dot(fm[:, TAPS:], prod[...])
    co[...] = dot(fm[:, :BLOCK], cig[...])
    for s in range(n):
        for kind in range(4):
            for d in range(2):
                gather_copy(s, kind, d).wait_send()

    h_re, h_im = hs.at[pl.ds(0, FREQ)], hs.at[pl.ds(FREQ, FREQ)]
    tail.wait_recv()
    halo = hx[...]
    xs[...] += dot(fm[:, :TAPS], jnp.where(ctx > 0, halo, jnp.zeros_like(halo)))
    x_re, x_im = xs.at[pl.ds(0, FREQ)], xs.at[pl.ds(FREQ, FREQ)]
    spec = jnp.concatenate(
        [x_re[...] * h_re[...] - x_im[...] * h_im[...], x_re[...] * h_im[...] + x_im[...] * h_re[...]], axis=0
    ).astype(BF)
    conv[...] = dot(im[:BLOCK, :], spec)
    G[0] = (og[...].astype(F32) * conv[...]).astype(BF)
    head.wait_recv()
    halo = hc[...]
    cs[...] = co[...] + dot(fm[:, BLOCK:], jnp.where(ctx < N_CTX - 1, halo, jnp.zeros_like(halo)))
    c_re, c_im = cs.at[pl.ds(0, FREQ)], cs.at[pl.ds(FREQ, FREQ)]
    spec = jnp.concatenate(
        [c_re[...] * h_re[...] + c_im[...] * h_im[...], c_im[...] * h_re[...] - c_re[...] * h_im[...]], axis=0
    ).astype(BF)
    back = dot(im[BLOCK : 2 * BLOCK, :], spec)
    G[1] = (back * qkv[2].astype(F32)).astype(BF)
    G[2] = (back * qkv[1].astype(F32)).astype(BF)

    def scatter_copy(s, kind, d):
        t = s % 2
        c0, kw = starts(SCATTER)[s], SCATTER[s]
        whole, half = pl.ds(c0, kw), pl.ds(c0 + d * (kw // 2), kw // 2)
        ahead = 1 if d == 0 else SIDE - 1
        if kind == 0:
            c, dim = coord(1 - t, 2), 1 - t
            src, dst = (PB.at[:, c, :, half] if t == 0 else PB.at[c, :, :, half]), R1H.at[:, :, half]
        elif kind == 1:
            c, dim = coord(1 - t, ahead), 1 - t
            src, dst = (PB.at[:, c, :, whole] if t == 0 else PB.at[c, :, :, whole]), R1.at[d, :, :, whole]
        elif kind == 2:
            c, dim = coord(t, 2), t
            src, dst = (PB.at[c, y, :, half] if t == 0 else PB.at[x, c, :, half]), R2H.at[:, half]
        else:
            c, dim = coord(t, ahead), t
            src, dst = (PB.at[c, y, :, whole] if t == 0 else PB.at[x, c, :, whole]), R2.at[d, :, whole]
        return pltpu.make_async_remote_copy(
            src_ref=src, dst_ref=dst, send_sem=rs_send.at[s, kind, d], recv_sem=rs_recv.at[s, kind, d],
            device_id=near(dim, d), device_id_type=MESH,
        )

    def produce(s):
        c0, kw = starts(SCATTER)[s], SCATTER[s]
        total = None
        for w in range(3):
            part = lax.dot_general(
                G[w], W[w, c0 : c0 + kw, :], (((1,), (1,)), ((), ())), preferred_element_type=F32
            )
            total = part if total is None else total + part
        PB[:, :, :, c0 : c0 + kw] = total.astype(BF).reshape(SIDE, SIDE, ROWS, kw)
        for d in range(2):
            scatter_copy(s, 0, d).start()

    def add_half_block(s):
        t = s % 2
        c0, kw = starts(SCATTER)[s], SCATTER[s]
        for d in range(2):
            half = slice(c0 + d * (kw // 2), c0 + (d + 1) * (kw // 2))
            c = coord(1 - t, 1 if d == 0 else SIDE - 1)
            scatter_copy(s, 0, d).wait_recv()
            got = R1H[:, :, half].astype(F32)
            if t == 0:
                PB[:, c, :, half] = (PB[:, c, :, half].astype(F32) + got).astype(BF)
            else:
                PB[c, :, :, half] = (PB[c, :, :, half].astype(F32) + got).astype(BF)
            scatter_copy(s, 1, d).start()

    def add_blocks(s):
        t = s % 2
        c0, kw = starts(SCATTER)[s], SCATTER[s]
        cols = slice(c0, c0 + kw)
        for d in range(2):
            scatter_copy(s, 1, d).wait_recv()
        got = R1[0, :, :, cols].astype(F32) + R1[1, :, :, cols].astype(F32)
        if t == 0:
            PB[:, y, :, cols] = (PB[:, y, :, cols].astype(F32) + got).astype(BF)
        else:
            PB[x, :, :, cols] = (PB[x, :, :, cols].astype(F32) + got).astype(BF)
        for d in range(2):
            scatter_copy(s, 2, d).start()

    def add_half_rows(s):
        t = s % 2
        c0, kw = starts(SCATTER)[s], SCATTER[s]
        for d in range(2):
            half = slice(c0 + d * (kw // 2), c0 + (d + 1) * (kw // 2))
            c = coord(t, 1 if d == 0 else SIDE - 1)
            scatter_copy(s, 2, d).wait_recv()
            got = R2H[:, half].astype(F32)
            if t == 0:
                PB[c, y, :, half] = (PB[c, y, :, half].astype(F32) + got).astype(BF)
            else:
                PB[x, c, :, half] = (PB[x, c, :, half].astype(F32) + got).astype(BF)
            scatter_copy(s, 3, d).start()

    def finish(s):
        c0, kw = starts(SCATTER)[s], SCATTER[s]
        cols = slice(c0, c0 + kw)
        for d in range(2):
            scatter_copy(s, 3, d).wait_recv()
        gout[:, cols] = (
            PB[x, y, :, cols].astype(F32) + R2[0, :, cols].astype(F32) + R2[1, :, cols].astype(F32)
        ).astype(BF)

    def piece_copy(k):
        to = (ctx + k) % N_CTX
        return pltpu.make_async_remote_copy(
            src_ref=fpart.at[to], dst_ref=FR.at[k], send_sem=f_send.at[0, k], recv_sem=f_recv.at[0, k],
            device_id={"ctx": to}, device_id_type=MESH,
        )

    def share_copy(k):
        return pltpu.make_async_remote_copy(
            src_ref=FO.at[ctx], dst_ref=FO.at[ctx], send_sem=f_send.at[1, k], recv_sem=f_recv.at[1, k],
            device_id={"ctx": (ctx + k) % N_CTX}, device_id_type=MESH,
        )

    def share_arrival(k):
        slot = (ctx + N_CTX - k) % N_CTX
        return pltpu.make_async_remote_copy(
            src_ref=FO.at[slot], dst_ref=FO.at[slot], send_sem=f_send.at[1, k], recv_sem=f_recv.at[1, k],
            device_id={"ctx": (ctx + k) % N_CTX}, device_id_type=MESH,
        )

    def filter_start():
        o_re, o_im = co.at[pl.ds(0, FREQ)], co.at[pl.ds(FREQ, FREQ)]
        spec = jnp.concatenate(
            [x_re[...] * o_re[...] + x_im[...] * o_im[...], x_im[...] * o_re[...] - x_re[...] * o_im[...]], axis=0
        ).astype(BF)
        fpart[...] = dot(im[2 * BLOCK :, :], spec).astype(BF).reshape(N_CTX, TAPS // N_CTX, GROUP)
        for k in range(1, N_CTX):
            piece_copy(k).start()

    def filter_sum():
        total = fpart[ctx].astype(F32)
        for k in range(1, N_CTX):
            piece_copy(k).wait_recv()
            total = total + FR[k].astype(F32)
        FO[ctx] = total.astype(BF)
        for k in range(1, N_CTX):
            share_copy(k).start()

    mixed_copy = pltpu.make_async_copy(mixed, mixed_out, out_sem.at[0])
    m = len(SCATTER)
    lag = 2
    for s in range(m + 4 * lag):
        if s < m:
            produce(s)
        for stage, fn in enumerate((add_half_block, add_blocks, add_half_rows, finish)):
            j = s - (stage + 1) * lag
            if 0 <= j < m:
                fn(j)
        if s == 3:
            filter_start()
        if s == 5:
            mixed[...] = (qkv[0].astype(F32) * conv[...]).astype(BF)
            mixed_copy.start()
        if s == 8:
            filter_sum()
    grad_copy = pltpu.make_async_copy(gout, grad_out, out_sem.at[1])
    grad_copy.start()
    for k in range(1, N_CTX):
        share_arrival(k).wait_recv()
    fout[...] = FO[...].astype(F32)
    filt_copy = pltpu.make_async_copy(fout, filt_out, out_sem.at[2])
    filt_copy.start()
    tail.wait_send()
    head.wait_send()
    for s in range(m):
        for kind in range(4):
            for d in range(2):
                scatter_copy(s, kind, d).wait_send()
    for k in range(1, N_CTX):
        piece_copy(k).wait_send()
        share_copy(k).wait_send()
    mixed_copy.wait()
    grad_copy.wait()
    filt_copy.wait()


def hand_on(*refs):
    held, load_sem, store_sem = refs[6:9], refs[9], refs[10]
    loads = [pltpu.make_async_copy(refs[i], held[i], load_sem.at[i]) for i in range(3)]
    stores = [pltpu.make_async_copy(held[i], refs[3 + i], store_sem.at[i]) for i in range(3)]
    for c in loads:
        c.start()
    for i in range(3):
        loads[i].wait()
        stores[i].start()
    for c in stores:
        c.wait()


def on_device(inputs, query_weight, key_weight, value_weight, filter_taps, out_grad):
    forward, inverse = transforms()
    vm, dma = pltpu.VMEM, pltpu.SemaphoreType.DMA
    n, m = len(GATHER), len(SCATTER)
    piece = TAPS // N_CTX
    mixed, grad, filt = pl.pallas_call(
        kernel,
        out_shape=(
            jax.ShapeDtypeStruct((BLOCK, GROUP), BF),
            jax.ShapeDtypeStruct((ROWS, D), BF),
            jax.ShapeDtypeStruct((N_CTX, piece, GROUP), F32),
        ),
        in_specs=[pl.BlockSpec(memory_space=pl.ANY)] * 8,
        out_specs=(pl.BlockSpec(memory_space=pl.ANY),) * 3,
        scratch_shapes=[
            vm((SIDE, SIDE, ROWS, D), BF),
            vm((3, D, GROUP), BF),
            vm((3, BLOCK, GROUP), F32),
            vm((BLOCK, GROUP), BF),
            vm((TAPS, GROUP), F32),
            vm((POINTS, POINTS), BF),
            vm((2 * BLOCK + TAPS, POINTS), BF),
            vm((3, BLOCK, GROUP), BF),
            vm((BLOCK, GROUP), BF),
            vm((BLOCK, GROUP), BF),
            vm((TAPS, GROUP), BF),
            vm((TAPS, GROUP), BF),
            vm((POINTS, GROUP), F32),
            vm((POINTS, GROUP), F32),
            vm((POINTS, GROUP), F32),
            vm((POINTS, GROUP), F32),
            vm((BLOCK, GROUP), F32),
            vm((3, BLOCK, GROUP), BF),
            vm((BLOCK, GROUP), BF),
            vm((SIDE, SIDE, ROWS, D), BF),
            vm((SIDE, ROWS, D), BF),
            vm((2, SIDE, ROWS, D), BF),
            vm((ROWS, D), BF),
            vm((2, ROWS, D), BF),
            vm((ROWS, D), BF),
            vm((N_CTX, piece, GROUP), BF),
            vm((N_CTX, piece, GROUP), BF),
            vm((N_CTX, piece, GROUP), BF),
            vm((N_CTX, piece, GROUP), F32),
            dma,
            dma((n, 3)),
            dma((4,)),
            dma((3,)),
            dma((n, 4, 2)),
            dma((n, 4, 2)),
            dma((2,)),
            dma((2,)),
            dma((m, 4, 2)),
            dma((m, 4, 2)),
            dma((2, N_CTX)),
            dma((2, N_CTX)),
            pltpu.SemaphoreType.REGULAR((3, 2)),
        ],
        compiler_params=pltpu.CompilerParams(
            collective_id=0, has_side_effects=True, vmem_limit_bytes=60 << 20
        ),
    )(inputs, query_weight, key_weight, value_weight, filter_taps, out_grad, forward, inverse)
    outs = (mixed, grad, filt.reshape(TAPS, GROUP))
    return pl.pallas_call(
        hand_on,
        out_shape=tuple(jax.ShapeDtypeStruct(v.shape, v.dtype) for v in outs),
        in_specs=[pl.BlockSpec(memory_space=pl.ANY)] * 3,
        out_specs=(pl.BlockSpec(memory_space=pl.ANY),) * 3,
        scratch_shapes=[*(vm(v.shape, v.dtype) for v in outs), dma((3,)), dma((3,))],
    )(*outs)


def solution(mesh):
    in_specs = (
        P(("ctx", "tp"), None),
        P(None, "tp"),
        P(None, "tp"),
        P(None, "tp"),
        P(None, "tp"),
        P("ctx", "tp"),
    )
    out_specs = (P("ctx", "tp"), P(("ctx", "tp"), None), P(None, "tp"))
    return jax.shard_map(
        on_device, mesh=mesh, in_specs=in_specs, out_specs=out_specs, check_vma=False
    )
```

```python
import jax
import jax.numpy as jnp
import numpy as np
from jax import lax
from jax.experimental import pallas as pl
from jax.experimental.pallas import tpu as pltpu
from jax.sharding import PartitionSpec as P

MESH = pl.DeviceIdType.MESH
BF, F32 = jnp.bfloat16, jnp.float32
SIDE = 4
ROWS = 16
D = 8192
GROUP = 512
BLOCK = 256
TAPS = 128
N_CTX = 8
FREQ = 192
POINTS = 2 * FREQ
GATHER = (2048, 2048, 2048, 2048)
SCATTER = (1024, 1024, 1536, 1536, 1536, 1536)


def starts(widths):
    return [sum(widths[:i]) for i in range(len(widths))]


def transforms():
    angle = np.pi / POINTS * np.outer(2 * np.arange(FREQ) + 1, np.arange(POINTS))
    forward = np.concatenate([np.cos(angle), -np.sin(angle)], axis=0)
    back = forward.T * (2.0 / POINTS)
    lags = TAPS - np.arange(TAPS)
    inverse = np.concatenate([back[TAPS:], back[:BLOCK], back[lags]], axis=0)
    return jnp.asarray(forward, BF), jnp.asarray(inverse, BF)


def dot(a, b):
    return jnp.dot(a, b, preferred_element_type=F32)


def kernel(
    inp, wq, wk, wv, taps_in, og_in, fwd_in, inv_in,
    mixed_out, grad_out, filt_out,
    X, W, acc, og, taps, fm, im, qkv, prod, cig, hx, hc, xs, hs, co, cs, conv, G,
    mixed, PB, R1H, R1, R2H, R2, gout, fpart, FR, FO, fout,
    own_sem, w_sem, in_sem, out_sem, ag_send, ag_recv, halo_send, halo_recv, rs_send, rs_recv,
    f_send, f_recv, met,
):
    ctx = lax.axis_index("ctx")
    tp = lax.axis_index("tp")
    x = tp // SIDE
    y = tp % SIDE

    def coord(dim, shift=0):
        return ((x if dim == 0 else y) + shift) % SIDE

    def near(dim, d):
        s = 1 if d == 0 else SIDE - 1
        if dim == 0:
            return {"tp": coord(0, s) * SIDE + y}
        return {"tp": x * SIDE + coord(1, s)}

    own_copies = [pltpu.make_async_copy(inp, X.at[x, y], own_sem)]
    loads = []
    for s, c0 in enumerate(starts(GATHER)):
        cols = pl.ds(c0, GATHER[s])
        loads.append([
            pltpu.make_async_copy(w.at[cols, :], W.at[i, cols, :], w_sem.at[s, i])
            for i, w in enumerate((wq, wk, wv))
        ])
    small = [
        pltpu.make_async_copy(src, dst, in_sem.at[i])
        for i, (src, dst) in enumerate(((fwd_in, fm), (taps_in, taps), (inv_in, im), (og_in, og)))
    ]
    own_copies[0].start()
    for c in small:
        c.start(priority=1)

    barrier = pltpu.get_barrier_semaphore()
    for dim in range(2):
        for d in range(2):
            pl.semaphore_signal(barrier, inc=1, device_id=near(dim, d), device_id_type=MESH)
    along = ({"ctx": (ctx + 1) % N_CTX}, {"ctx": (ctx + N_CTX - 1) % N_CTX})
    for to in along:
        pl.semaphore_signal(barrier, inc=1, device_id=to, device_id_type=MESH)
    pl.semaphore_wait(barrier, 6)

    def greet(r):
        for d, to in enumerate(along):
            pl.semaphore_signal(met.at[r, d], inc=1, device_id=to, device_id_type=MESH)

    def greeted(r):
        for d in range(2):
            pl.semaphore_wait(met.at[r, d], 1)

    own_copies[0].wait()

    def gather_copy(s, kind, d):
        t = s % 2
        c0, kw = starts(GATHER)[s], GATHER[s]
        whole, half = pl.ds(c0, kw), pl.ds(c0 + d * (kw // 2), kw // 2)
        back = SIDE - 1 if d == 0 else 1
        if kind == 0:
            ref, dim = X.at[x, y, :, whole], t
        elif kind == 1:
            c = coord(t, back)
            ref, dim = (X.at[c, y, :, half] if t == 0 else X.at[x, c, :, half]), t
        elif kind == 2:
            ref, dim = (X.at[:, y, :, whole] if t == 0 else X.at[x, :, :, whole]), 1 - t
        else:
            c = coord(1 - t, back)
            ref, dim = (X.at[:, c, :, half] if t == 0 else X.at[c, :, :, half]), 1 - t
        return pltpu.make_async_remote_copy(
            src_ref=ref, dst_ref=ref, send_sem=ag_send.at[s, kind, d], recv_sem=ag_recv.at[s, kind, d],
            device_id=near(dim, d), device_id_type=MESH,
        )

    def gather_stage(s, kind):
        for d in range(2):
            if kind in (1, 3):
                gather_copy(s, kind - 1, d).wait_recv()
            gather_copy(s, kind, d).start()

    def gather_wait(s, kind):
        for d in range(2):
            gather_copy(s, kind, d).wait_recv()

    def project(s, first, last):
        c0, kw = starts(GATHER)[s], GATHER[s]

        def one(w, carry):
            part = dot(X[:, :, :, c0 : c0 + kw].reshape(BLOCK, kw), W[w, c0 : c0 + kw, :])
            if s == 0:
                acc[w] = part
            else:
                acc[w] += part
            return carry

        lax.fori_loop(first, last, one, 0)

    n = len(GATHER)
    for s in range(n):
        gather_stage(s, 0)
    greet(0)
    for group in loads:
        for c in group:
            c.start(priority=1)
    for s in range(n):
        gather_stage(s, 1)
        if s >= 2:
            gather_wait(s - 2, 1)
            gather_stage(s - 2, 2)
    for s in (n - 2, n - 1):
        gather_wait(s, 1)
        gather_stage(s, 2)
    greeted(0)
    greet(1)
    for c in small:
        c.wait()
    tap = taps[...]
    tap_hi = tap.astype(BF)
    tap_lo = (tap - tap_hi.astype(F32)).astype(BF)
    hs[...] = dot(fm[:, :TAPS], tap_hi) + dot(fm[:, :TAPS], tap_lo)
    gather_stage(0, 3)
    gather_stage(1, 3)
    greeted(1)
    greet(2)
    for s in range(n):
        if s + 2 < n:
            gather_stage(s + 2, 3)
        gather_wait(s, 3)
        for c in loads[s]:
            c.wait()
        project(s, 0 if s < n - 2 else 1, 3)

    greeted(2)

    qkv[1] = acc[1].astype(BF)
    qkv[2] = acc[2].astype(BF)
    prod[...] = (qkv[1].astype(F32) * qkv[2].astype(F32)).astype(BF)
    tail = pltpu.make_async_remote_copy(
        src_ref=prod.at[pl.ds(BLOCK - TAPS, TAPS)], dst_ref=hx, send_sem=halo_send.at[0], recv_sem=halo_recv.at[0],
        device_id={"ctx": (ctx + 1) % N_CTX}, device_id_type=MESH,
    )
    tail.start()
    for s in (n - 2, n - 1):
        project(s, 0, 1)
    qkv[0] = acc[0].astype(BF)
    cig[...] = (og[...].astype(F32) * qkv[0].astype(F32)).astype(BF)
    head = pltpu.make_async_remote_copy(
        src_ref=cig.at[pl.ds(0, TAPS)], dst_ref=hc, send_sem=halo_send.at[1], recv_sem=halo_recv.at[1],
        device_id={"ctx": (ctx + N_CTX - 1) % N_CTX}, device_id_type=MESH,
    )
    head.start()
    xs[...] = dot(fm[:, TAPS:], prod[...])
    co[...] = dot(fm[:, :BLOCK], cig[...])
    for s in range(n):
        for kind in range(4):
            for d in range(2):
                gather_copy(s, kind, d).wait_send()

    h_re, h_im = hs.at[pl.ds(0, FREQ)], hs.at[pl.ds(FREQ, FREQ)]
    tail.wait_recv()
    halo = hx[...]
    xs[...] += dot(fm[:, :TAPS], jnp.where(ctx > 0, halo, jnp.zeros_like(halo)))
    x_re, x_im = xs.at[pl.ds(0, FREQ)], xs.at[pl.ds(FREQ, FREQ)]
    spec = jnp.concatenate(
        [x_re[...] * h_re[...] - x_im[...] * h_im[...], x_re[...] * h_im[...] + x_im[...] * h_re[...]], axis=0
    ).astype(BF)
    conv[...] = dot(im[:BLOCK, :], spec)
    G[0] = (og[...].astype(F32) * conv[...]).astype(BF)
    head.wait_recv()
    halo = hc[...]
    cs[...] = co[...] + dot(fm[:, BLOCK:], jnp.where(ctx < N_CTX - 1, halo, jnp.zeros_like(halo)))
    c_re, c_im = cs.at[pl.ds(0, FREQ)], cs.at[pl.ds(FREQ, FREQ)]
    spec = jnp.concatenate(
        [c_re[...] * h_re[...] + c_im[...] * h_im[...], c_im[...] * h_re[...] - c_re[...] * h_im[...]], axis=0
    ).astype(BF)
    back = dot(im[BLOCK : 2 * BLOCK, :], spec)
    G[1] = (back * qkv[2].astype(F32)).astype(BF)
    G[2] = (back * qkv[1].astype(F32)).astype(BF)

    def scatter_copy(s, kind, d):
        t = s % 2
        c0, kw = starts(SCATTER)[s], SCATTER[s]
        whole, half = pl.ds(c0, kw), pl.ds(c0 + d * (kw // 2), kw // 2)
        ahead = 1 if d == 0 else SIDE - 1
        if kind == 0:
            c, dim = coord(1 - t, 2), 1 - t
            src, dst = (PB.at[:, c, :, half] if t == 0 else PB.at[c, :, :, half]), R1H.at[:, :, half]
        elif kind == 1:
            c, dim = coord(1 - t, ahead), 1 - t
            src, dst = (PB.at[:, c, :, whole] if t == 0 else PB.at[c, :, :, whole]), R1.at[d, :, :, whole]
        elif kind == 2:
            c, dim = coord(t, 2), t
            src, dst = (PB.at[c, y, :, half] if t == 0 else PB.at[x, c, :, half]), R2H.at[:, half]
        else:
            c, dim = coord(t, ahead), t
            src, dst = (PB.at[c, y, :, whole] if t == 0 else PB.at[x, c, :, whole]), R2.at[d, :, whole]
        return pltpu.make_async_remote_copy(
            src_ref=src, dst_ref=dst, send_sem=rs_send.at[s, kind, d], recv_sem=rs_recv.at[s, kind, d],
            device_id=near(dim, d), device_id_type=MESH,
        )

    def produce(s):
        c0, kw = starts(SCATTER)[s], SCATTER[s]
        total = None
        for w in range(3):
            part = lax.dot_general(
                G[w], W[w, c0 : c0 + kw, :], (((1,), (1,)), ((), ())), preferred_element_type=F32
            )
            total = part if total is None else total + part
        PB[:, :, :, c0 : c0 + kw] = total.astype(BF).reshape(SIDE, SIDE, ROWS, kw)
        for d in range(2):
            scatter_copy(s, 0, d).start()

    def add_half_block(s):
        t = s % 2
        c0, kw = starts(SCATTER)[s], SCATTER[s]
        for d in range(2):
            half = slice(c0 + d * (kw // 2), c0 + (d + 1) * (kw // 2))
            c = coord(1 - t, 1 if d == 0 else SIDE - 1)
            scatter_copy(s, 0, d).wait_recv()
            got = R1H[:, :, half].astype(F32)
            if t == 0:
                PB[:, c, :, half] = (PB[:, c, :, half].astype(F32) + got).astype(BF)
            else:
                PB[c, :, :, half] = (PB[c, :, :, half].astype(F32) + got).astype(BF)
            scatter_copy(s, 1, d).start()

    def add_blocks(s):
        t = s % 2
        c0, kw = starts(SCATTER)[s], SCATTER[s]
        cols = slice(c0, c0 + kw)
        for d in range(2):
            scatter_copy(s, 1, d).wait_recv()
        got = R1[0, :, :, cols].astype(F32) + R1[1, :, :, cols].astype(F32)
        if t == 0:
            PB[:, y, :, cols] = (PB[:, y, :, cols].astype(F32) + got).astype(BF)
        else:
            PB[x, :, :, cols] = (PB[x, :, :, cols].astype(F32) + got).astype(BF)
        for d in range(2):
            scatter_copy(s, 2, d).start()

    def add_half_rows(s):
        t = s % 2
        c0, kw = starts(SCATTER)[s], SCATTER[s]
        for d in range(2):
            half = slice(c0 + d * (kw // 2), c0 + (d + 1) * (kw // 2))
            c = coord(t, 1 if d == 0 else SIDE - 1)
            scatter_copy(s, 2, d).wait_recv()
            got = R2H[:, half].astype(F32)
            if t == 0:
                PB[c, y, :, half] = (PB[c, y, :, half].astype(F32) + got).astype(BF)
            else:
                PB[x, c, :, half] = (PB[x, c, :, half].astype(F32) + got).astype(BF)
            scatter_copy(s, 3, d).start()

    def finish(s):
        c0, kw = starts(SCATTER)[s], SCATTER[s]
        cols = slice(c0, c0 + kw)
        for d in range(2):
            scatter_copy(s, 3, d).wait_recv()
        gout[:, cols] = (
            PB[x, y, :, cols].astype(F32) + R2[0, :, cols].astype(F32) + R2[1, :, cols].astype(F32)
        ).astype(BF)

    def piece_copy(k):
        to = (ctx + k) % N_CTX
        return pltpu.make_async_remote_copy(
            src_ref=fpart.at[to], dst_ref=FR.at[k], send_sem=f_send.at[0, k], recv_sem=f_recv.at[0, k],
            device_id={"ctx": to}, device_id_type=MESH,
        )

    def share_copy(k):
        return pltpu.make_async_remote_copy(
            src_ref=FO.at[ctx], dst_ref=FO.at[ctx], send_sem=f_send.at[1, k], recv_sem=f_recv.at[1, k],
            device_id={"ctx": (ctx + k) % N_CTX}, device_id_type=MESH,
        )

    def share_arrival(k):
        slot = (ctx + N_CTX - k) % N_CTX
        return pltpu.make_async_remote_copy(
            src_ref=FO.at[slot], dst_ref=FO.at[slot], send_sem=f_send.at[1, k], recv_sem=f_recv.at[1, k],
            device_id={"ctx": (ctx + k) % N_CTX}, device_id_type=MESH,
        )

    def filter_start():
        o_re, o_im = co.at[pl.ds(0, FREQ)], co.at[pl.ds(FREQ, FREQ)]
        spec = jnp.concatenate(
            [x_re[...] * o_re[...] + x_im[...] * o_im[...], x_im[...] * o_re[...] - x_re[...] * o_im[...]], axis=0
        ).astype(BF)
        fpart[...] = dot(im[2 * BLOCK :, :], spec).astype(BF).reshape(N_CTX, TAPS // N_CTX, GROUP)
        for k in range(1, N_CTX):
            piece_copy(k).start()

    def filter_sum():
        total = fpart[ctx].astype(F32)
        for k in range(1, N_CTX):
            piece_copy(k).wait_recv()
            total = total + FR[k].astype(F32)
        FO[ctx] = total.astype(BF)
        for k in range(1, N_CTX):
            share_copy(k).start()

    mixed_copy = pltpu.make_async_copy(mixed, mixed_out, out_sem.at[0])
    m = len(SCATTER)
    lag = 2
    for s in range(m + 4 * lag):
        if s < m:
            produce(s)
        for stage, fn in enumerate((add_half_block, add_blocks, add_half_rows, finish)):
            j = s - (stage + 1) * lag
            if 0 <= j < m:
                fn(j)
        if s == 3:
            filter_start()
        if s == 5:
            mixed[...] = (qkv[0].astype(F32) * conv[...]).astype(BF)
            mixed_copy.start()
        if s == 8:
            filter_sum()
    grad_copy = pltpu.make_async_copy(gout, grad_out, out_sem.at[1])
    grad_copy.start()
    for k in range(1, N_CTX):
        share_arrival(k).wait_recv()
    fout[...] = FO[...].astype(F32)
    filt_copy = pltpu.make_async_copy(fout, filt_out, out_sem.at[2])
    filt_copy.start()
    tail.wait_send()
    head.wait_send()
    for s in range(m):
        for kind in range(4):
            for d in range(2):
                scatter_copy(s, kind, d).wait_send()
    for k in range(1, N_CTX):
        piece_copy(k).wait_send()
        share_copy(k).wait_send()
    mixed_copy.wait()
    grad_copy.wait()
    filt_copy.wait()


def hand_on(*refs):
    held, load_sem, store_sem = refs[6:9], refs[9], refs[10]
    loads = [pltpu.make_async_copy(refs[i], held[i], load_sem.at[i]) for i in range(3)]
    stores = [pltpu.make_async_copy(held[i], refs[3 + i], store_sem.at[i]) for i in range(3)]
    for c in loads:
        c.start()
    for i in range(3):
        loads[i].wait()
        stores[i].start()
    for c in stores:
        c.wait()


def on_device(inputs, query_weight, key_weight, value_weight, filter_taps, out_grad):
    forward, inverse = transforms()
    vm, dma = pltpu.VMEM, pltpu.SemaphoreType.DMA
    n, m = len(GATHER), len(SCATTER)
    piece = TAPS // N_CTX
    mixed, grad, filt = pl.pallas_call(
        kernel,
        out_shape=(
            jax.ShapeDtypeStruct((BLOCK, GROUP), BF),
            jax.ShapeDtypeStruct((ROWS, D), BF),
            jax.ShapeDtypeStruct((N_CTX, piece, GROUP), F32),
        ),
        in_specs=[pl.BlockSpec(memory_space=pl.ANY)] * 8,
        out_specs=(pl.BlockSpec(memory_space=pl.ANY),) * 3,
        scratch_shapes=[
            vm((SIDE, SIDE, ROWS, D), BF),
            vm((3, D, GROUP), BF),
            vm((3, BLOCK, GROUP), F32),
            vm((BLOCK, GROUP), BF),
            vm((TAPS, GROUP), F32),
            vm((POINTS, POINTS), BF),
            vm((2 * BLOCK + TAPS, POINTS), BF),
            vm((3, BLOCK, GROUP), BF),
            vm((BLOCK, GROUP), BF),
            vm((BLOCK, GROUP), BF),
            vm((TAPS, GROUP), BF),
            vm((TAPS, GROUP), BF),
            vm((POINTS, GROUP), F32),
            vm((POINTS, GROUP), F32),
            vm((POINTS, GROUP), F32),
            vm((POINTS, GROUP), F32),
            vm((BLOCK, GROUP), F32),
            vm((3, BLOCK, GROUP), BF),
            vm((BLOCK, GROUP), BF),
            vm((SIDE, SIDE, ROWS, D), BF),
            vm((SIDE, ROWS, D), BF),
            vm((2, SIDE, ROWS, D), BF),
            vm((ROWS, D), BF),
            vm((2, ROWS, D), BF),
            vm((ROWS, D), BF),
            vm((N_CTX, piece, GROUP), BF),
            vm((N_CTX, piece, GROUP), BF),
            vm((N_CTX, piece, GROUP), BF),
            vm((N_CTX, piece, GROUP), F32),
            dma,
            dma((n, 3)),
            dma((4,)),
            dma((3,)),
            dma((n, 4, 2)),
            dma((n, 4, 2)),
            dma((2,)),
            dma((2,)),
            dma((m, 4, 2)),
            dma((m, 4, 2)),
            dma((2, N_CTX)),
            dma((2, N_CTX)),
            pltpu.SemaphoreType.REGULAR((3, 2)),
        ],
        compiler_params=pltpu.CompilerParams(
            collective_id=0, has_side_effects=True, vmem_limit_bytes=60 << 20
        ),
    )(inputs, query_weight, key_weight, value_weight, filter_taps, out_grad, forward, inverse)
    outs = (mixed, grad, filt.reshape(TAPS, GROUP))
    return pl.pallas_call(
        hand_on,
        out_shape=tuple(jax.ShapeDtypeStruct(v.shape, v.dtype) for v in outs),
        in_specs=[pl.BlockSpec(memory_space=pl.ANY)] * 3,
        out_specs=(pl.BlockSpec(memory_space=pl.ANY),) * 3,
        scratch_shapes=[*(vm(v.shape, v.dtype) for v in outs), dma((3,)), dma((3,))],
    )(*outs)


def solution(mesh):
    in_specs = (
        P(("ctx", "tp"), None),
        P(None, "tp"),
        P(None, "tp"),
        P(None, "tp"),
        P(None, "tp"),
        P("ctx", "tp"),
    )
    out_specs = (P("ctx", "tp"), P(("ctx", "tp"), None), P(None, "tp"))
    return jax.shard_map(
        on_device, mesh=mesh, in_specs=in_specs, out_specs=out_specs, check_vma=False
    )
```
